32 devices in a mesh: grp: 2 (over x), ha: 8 (over z, y), col: 2 (over core).
Axes of the slice: x: 2, y: 2, z: 4, core: 2. Of those that a mesh axis runs over, the one named last changes fastest.
Arguments:
- latent: bfloat16 [2, 64, 128, 384], P('grp', 'ha', None, 'col'), parts along dimension 0, may hold values from -6 to 6
- up_weight: bfloat16 [4, 4, 384, 192], replicated, may hold values from -0.15625 to 0.15625
- conv_one: bfloat16 [3, 3, 192, 192], replicated, may hold values from -0.15625 to 0.15625
- gain_one: float32 [192], replicated, may hold values from 0.1 to 1.9
- conv_two: bfloat16 [3, 3, 192, 192], replicated, may hold values from -0.15625 to 0.15625
- gain_two: float32 [192], replicated, may hold values from 0.1 to 1.9
Outputs:
- decoded: bfloat16 [2, 128, 256, 192], P('grp', 'ha', 'col'), parts along dimension 0
The draws below stay inside these ranges and needn't reach their ends.
There are 2 independent parts, one for each index of `grp`. The reference program is written for one: setup_inputs(seed, part) draws one part's arguments, and reference() takes and returns one part's arrays. A program takes and returns all parts, laid end to end along the dimension named above; an argument that names none is the same for every part. Nothing has to cross between parts.
All inputs are finite; a program needn't handle non-finite values.
Results may differ from the reference program's by a relative error of at most 0.008.
Values may be sent and summed in bfloat16 or wider, within the bound.
A program may use at most 64 MiB of HBM per device.

```python
import jax
import jax.numpy as jnp
from jax import lax

CI = 384
C = 192
F = 1
W = 128
H = 64


def shard_levels(rng, shape, cuts, low, high):
    level, own = 1.0, jax.random.fold_in(rng, 6)
    for position, parts in cuts:
        heights = jnp.exp(jax.random.uniform(jax.random.fold_in(own, position), (parts,), jnp.float32, low / len(cuts), high / len(cuts)))
        level = level * jnp.repeat(heights, shape[position] // parts).reshape([-1 if axis == position else 1 for axis in range(len(shape))])
    return level


def noise(rng, extent, scale, most, pieces=(), kind=jnp.bfloat16):
    result = scale * jax.random.normal(rng, extent, jnp.float32)
    if pieces:
        result = result * shard_levels(rng, extent, pieces, -0.22, 0.18)
    return jnp.clip(result, -most, most).astype(kind)


def setup_inputs(seed: int = 0, part: int = 0) -> dict:
    keys = jax.random.split(jax.random.key(seed), 7)
    part_splits = jax.random.split(jax.random.fold_in(keys[6], part), 7)
    return {
        "latent": noise(part_splits[0], (F, H, W, CI), 1.0, 6.0, ((1, 8), (3, 2))),
        "up_weight": noise(keys[1], (4, 4, CI, C), (4 * CI) ** -0.5, 0.15625),
        "conv_one": noise(keys[2], (3, 3, C, C), (9 * C) ** -0.5, 0.15625),
        "gain_one": jnp.clip(1.0 + 0.18 * jax.random.normal(keys[3], (C,), jnp.float32), 0.1, 1.9),
        "conv_two": noise(keys[4], (3, 3, C, C), (9 * C) ** -0.5, 0.15625),
        "gain_two": jnp.clip(1.0 + 0.18 * jax.random.normal(keys[5], (C,), jnp.float32), 0.1, 1.9),
    }


phase_taps = (((0, 1), (-1, 3)), ((0, 2), (1, 0)))

def upsample_exact(padded, kernel):
    row_count = padded.shape[1] - 2
    col_count = padded.shape[2] - 2
    wide_input = padded.astype(jnp.float32)
    wide_kernel = kernel.astype(jnp.float32)
    phase_rows = []
    for row_phase in range(2):
        phase_cols = []
        for col_phase in range(2):
            summed = None
            for row_shift, row_tap in phase_taps[row_phase]:
                for col_shift, col_tap in phase_taps[col_phase]:
                    window = wide_input[:, 1 + row_shift:1 + row_shift + row_count, 1 + col_shift:1 + col_shift + col_count, :]
                    product = jnp.einsum('fhwc,cd->fhwd', window, wide_kernel[row_tap, col_tap])
                    summed = product if summed is None else summed + product
            phase_cols.append(summed)
        phase_rows.append(jnp.stack(phase_cols, axis=3))
    joined = jnp.stack(phase_rows, axis=2)
    return joined.reshape(joined.shape[0], 2 * row_count, 2 * col_count, joined.shape[-1])

def activate(field, gain):
    wide = field.astype(jnp.float32)
    stats = lax.optimization_barrier(jnp.mean(wide * wide, axis=-1, keepdims=True))
    normed = wide * lax.rsqrt(stats + 1e-06) * gain
    return jax.nn.silu(normed).astype(jnp.bfloat16)

def convolve(field, weight):
    padded = jnp.pad(field, ((0, 0), (1, 1), (1, 1), (0, 0)))
    return lax.conv_general_dilated(padded.astype(jnp.float32), weight.astype(jnp.float32), (1, 1), 'VALID', dimension_numbers=('NHWC', 'HWIO', 'NHWC'))

def reference(latent, up_weight, conv_one, gain_one, conv_two, gain_two):
    padded = jnp.pad(latent, ((0, 0), (1, 1), (1, 1), (0, 0)))
    upsampled = upsample_exact(padded, up_weight).astype(jnp.bfloat16)
    first_act = activate(upsampled, gain_one)
    hidden = convolve(first_act, conv_one).astype(jnp.bfloat16)
    second_act = activate(hidden, gain_two)
    return (upsampled.astype(jnp.float32) + convolve(second_act, conv_two)).astype(jnp.bfloat16)
```

```python
import functools

import jax
import jax.numpy as jnp
from jax import lax
from jax.experimental import pallas as pl
from jax.experimental.pallas import tpu as pltpu
from jax.sharding import PartitionSpec as P

f32 = jnp.float32
bf16 = jnp.bfloat16
MESH = pl.DeviceIdType.MESH
STRIPS = 16
PAD = 16
phase_taps = (((0, 1), (-1, 3)), ((0, 2), (1, 0)))


def exchange_kernel(ha_count, lat, beside, above, below, send, recv):
    ha = lax.axis_index("ha")
    col = lax.axis_index("col")
    rows, width = lat.shape[1], lat.shape[2]
    window = width // 2 + PAD
    other = 1 - col

    def columns(core):
        return pl.ds(pl.multiple_of(core * (width // 2 - PAD), PAD), window)

    barrier = pltpu.get_barrier_semaphore()
    pl.semaphore_signal(barrier, 1, device_id={"col": other}, device_id_type=MESH)

    @pl.when(ha > 0)
    def _():
        for core in (0, 1):
            pl.semaphore_signal(
                barrier, 1, device_id={"ha": ha - 1, "col": core}, device_id_type=MESH
            )

    @pl.when(ha < ha_count - 1)
    def _():
        for core in (0, 1):
            pl.semaphore_signal(
                barrier, 1, device_id={"ha": ha + 1, "col": core}, device_id_type=MESH
            )

    peers = 1 + 2 * jnp.minimum(ha, 1) + 2 * jnp.minimum(ha_count - 1 - ha, 1)
    pl.semaphore_wait(barrier, peers)

    def copy(first, count, core, target, dst, sem):
        return pltpu.make_async_remote_copy(
            src_ref=lat.at[0, pl.ds(first, count), columns(core)],
            dst_ref=dst,
            send_sem=send.at[sem],
            recv_sem=recv.at[sem],
            device_id=target,
            device_id_type=MESH,
        )

    down = [
        copy(rows - 2, 2, core, {"ha": ha + 1, "col": core}, above.at[slot], 1 + slot)
        for slot, core in ((0, col), (1, other))
    ]
    up = [
        copy(0, 2, core, {"ha": ha - 1, "col": core}, below.at[slot], 3 + slot)
        for slot, core in ((0, col), (1, other))
    ]
    side = copy(0, rows, other, {"col": other}, beside, 0)

    @pl.when(ha < ha_count - 1)
    def _():
        for item in down:
            item.start()

    @pl.when(ha > 0)
    def _():
        for item in up:
            item.start()

    side.start()
    side.wait()

    @pl.when(ha < ha_count - 1)
    def _():
        for item in down:
            item.wait_send()
        for item in up:
            item.wait_recv()

    @pl.when(ha > 0)
    def _():
        for item in up:
            item.wait_send()
        for item in down:
            item.wait_recv()


def activate(wide, half_gain):
    stats = jnp.sum(wide * wide, axis=-1, keepdims=True) * (1.0 / wide.shape[-1])
    half = wide * lax.rsqrt(stats + 1e-06) * half_gain
    return (half * jnp.tanh(half) + half).astype(bf16)


def block_kernel(
    ha_count, lat, beside, above, below, gain_one, gain_two, up_hbm, one_hbm, two_hbm, out,
    up_w, one_w, two_w, spread, strips, ups, first, second, rows_f32, sem
):
    ha = lax.axis_index("ha")
    col = lax.axis_index("col")
    share = lat.shape[3]
    chans = out.shape[3]
    rows, width = lat.shape[1], lat.shape[2]
    window = width // 2 + PAD
    ql = width // 2 // STRIPS
    q = 2 * ql
    depth = 2 * share
    wide = first.shape[3]
    tiles = depth // 128

    copies = []
    for rp in range(2):
        for cp in range(2):
            tap = 0
            for _, ra in phase_taps[rp]:
                for _, cb in phase_taps[cp]:
                    for part, core in ((0, col), (1, 1 - col)):
                        copies.append(pltpu.make_async_copy(
                            up_hbm.at[ra, cb, pl.ds(pl.multiple_of(core * share, share), share)],
                            up_w.at[rp, cp, pl.ds(tap * depth + part * share, share)],
                            sem.at[0],
                        ))
                    tap += 1
    for number, (src, dst) in enumerate(((one_hbm, one_w), (two_hbm, two_w))):
        for a in range(3):
            for b in range(3):
                copies.append(pltpu.make_async_copy(
                    src.at[a, b],
                    dst.at[pl.ds((3 * a + b) * wide, chans)],
                    sem.at[1 + number],
                ))
    for item in copies:
        item.start()

    for w in (one_w, two_w):
        for n in range(9):
            w[pl.ds(n * wide + chans, wide - chans), :] = jnp.zeros((wide - chans, chans), bf16)

    zero_edge = jnp.zeros((PAD, 128), f32)
    for i in range(rows + 4):
        if i < 2:
            own, far = above[0, i], above[1, i]
        elif i < rows + 2:
            own = lat[0, i - 2, pl.ds(pl.multiple_of(col * (width // 2 - PAD), PAD), window)]
            far = beside[i - 2]
        else:
            own, far = below[0, i - rows - 2], below[1, i - rows - 2]
        own, far = own.astype(f32), far.astype(f32)
        full = jnp.concatenate([own, far], axis=-1)
        if i < 2:
            full = jnp.where(ha > 0, full, 0.0)
        elif i >= rows + 2:
            full = jnp.where(ha < ha_count - 1, full, 0.0)
        for k in range(tiles):
            spread[i, k, pl.ds(0, PAD)] = zero_edge
            spread[i, k, pl.ds(PAD + window, PAD)] = zero_edge
            spread[i, k, pl.ds(PAD, window)] = full[:, k * 128 : (k + 1) * 128]
    base = PAD + PAD * col
    for i in range(rows + 4):
        for t in range(ql + 4):
            for k in range(tiles):
                strips[i, t, :, pl.ds(k * 128, 128)] = spread[
                    i, k, pl.ds(base + t - 2, STRIPS, stride=ql), :
                ].astype(bf16)

    first[:, :, :, pl.ds(chans, wide - chans)] = jnp.zeros(
        first.shape[:3] + (wide - chans,), bf16
    )
    second[:, :, :, pl.ds(chans, wide - chans)] = jnp.zeros(
        second.shape[:3] + (wide - chans,), bf16
    )
    half_one = gain_one[...] * 0.5
    half_two = gain_two[...] * 0.5

    for item in copies[:32]:
        item.wait()

    block = 5
    nt = ql + 2
    for rp in range(2):
        for cp in range(2):
            def up_body(n, carry, rp=rp, cp=cp):
                pieces = []
                for dr, _ in phase_taps[rp]:
                    for dc, _ in phase_taps[cp]:
                        pieces.append(
                            strips[pl.ds(n * block + 1 + dr, block), pl.ds(1 + dc, nt)].reshape(
                                block * nt * STRIPS, depth
                            )
                        )
                lhs = jnp.concatenate(pieces, axis=-1)
                result = jnp.dot(lhs, up_w[rp, cp], preferred_element_type=f32).astype(bf16)
                act = activate(result.astype(f32), half_one)
                result = result.reshape(block, nt, STRIPS, chans)
                act = act.reshape(block, nt, STRIPS, chans)
                for u in range(block):
                    for t in range(nt):
                        r = 2 * (n * block + u) + rp
                        ups[r, 2 * t + cp] = result[u, t]
                        first[r, 2 * t + cp, :, pl.ds(0, chans)] = act[u, t]
                return carry

            lax.fori_loop(0, (rows + 2) // block, up_body, 0)

    strip = lax.broadcasted_iota(jnp.int32, (STRIPS, wide), 0)
    low = (strip == 0) & (col == 0)
    high = (strip == STRIPS - 1) & (col == 1)

    def clear(ref, rim):
        count, cols = ref.shape[0], ref.shape[1]

        def clear_row(r, carry):
            for t in range(rim):
                ref[r, t] = jnp.where(low, 0.0, ref[r, t].astype(f32)).astype(bf16)
                e = cols - rim + t
                ref[r, e] = jnp.where(high, 0.0, ref[r, e].astype(f32)).astype(bf16)
            return carry

        lax.fori_loop(0, count, clear_row, 0)

        @pl.when(ha == 0)
        def _():
            ref[pl.ds(0, rim)] = jnp.zeros((rim,) + ref.shape[1:], bf16)

        @pl.when(ha == ha_count - 1)
        def _():
            ref[pl.ds(count - rim, rim)] = jnp.zeros((rim,) + ref.shape[1:], bf16)

    clear(first, 2)

    def windows(ref, start, count, cols):
        return jnp.concatenate(
            [
                ref[pl.ds(start + a, count), pl.ds(b, cols)].reshape(count * cols * STRIPS, wide)
                for a in range(3)
                for b in range(3)
            ],
            axis=-1,
        )

    for item in copies[32:41]:
        item.wait()

    def one_body(n, carry):
        count = 3
        lhs = windows(first, n * count, count, q + 2)
        hidden = jnp.dot(lhs, one_w[...], preferred_element_type=f32).astype(bf16)
        act = activate(hidden.astype(f32), half_two)
        second[pl.ds(n * count, count), :, :, pl.ds(0, chans)] = act.reshape(
            count, q + 2, STRIPS, chans
        )
        return carry

    lax.fori_loop(0, (2 * rows + 2) // 3, one_body, 0)
    clear(second, 1)

    for item in copies[41:]:
        item.wait()

    def two_body(n, carry):
        count = 4
        lhs = windows(second, n * count, count, q)
        total = jnp.dot(lhs, two_w[...], preferred_element_type=f32)
        total = total.reshape(count, q, STRIPS, chans)
        for u in range(count):
            for t in range(q):
                value = total[u, t] + ups[n * count + u + 2, t + 2].astype(f32)
                rows_f32[0, u, pl.ds(t, STRIPS, stride=q), :] = value[:, :128]
                rows_f32[1, u, pl.ds(t, STRIPS, stride=q), pl.ds(0, chans - 128)] = value[:, 128:]
        for u in range(count):
            out[0, n * count + u, :, pl.ds(0, 128)] = rows_f32[0, u].astype(bf16)
            out[0, n * count + u, :, pl.ds(128, chans - 128)] = rows_f32[
                1, u, :, pl.ds(0, chans - 128)
            ].astype(bf16)
        return carry

    lax.fori_loop(0, 2 * rows // 4, two_body, 0)


def local(ha_count, latent, up_weight, conv_one, gain_one, conv_two, gain_two):
    _, rows, width, share = latent.shape
    chans = conv_one.shape[3]
    window = width // 2 + PAD
    wide = -(-chans // 256) * 256
    ql = width // 2 // STRIPS
    q = 2 * ql
    shapes = [(rows, window, share), (2, 2, window, share), (2, 2, window, share)]
    anywhere = pl.BlockSpec(memory_space=pl.ANY)
    beside, above, below = pl.pallas_call(
        functools.partial(exchange_kernel, ha_count),
        out_shape=[jax.ShapeDtypeStruct(s, bf16) for s in shapes],
        in_specs=[anywhere],
        out_specs=[anywhere] * 3,
        scratch_shapes=[pltpu.SemaphoreType.DMA((5,)), pltpu.SemaphoreType.DMA((5,))],
        compiler_params=pltpu.CompilerParams(collective_id=0, has_side_effects=True),
    )(latent)
    vmem = pl.BlockSpec(memory_space=pltpu.VMEM)
    return pl.pallas_call(
        functools.partial(block_kernel, ha_count),
        out_shape=jax.ShapeDtypeStruct((1, 2 * rows, width, chans), bf16),
        in_specs=[vmem] * 6 + [anywhere] * 3,
        out_specs=vmem,
        scratch_shapes=[
            pltpu.VMEM((2, 2, 8 * share, chans), bf16),
            pltpu.VMEM((9 * wide, chans), bf16),
            pltpu.VMEM((9 * wide, chans), bf16),
            pltpu.VMEM((rows + 4, 2 * share // 128, window + 2 * PAD, 128), f32),
            pltpu.VMEM((rows + 4, ql + 4, STRIPS, 2 * share), bf16),
            pltpu.VMEM((2 * rows + 4, q + 4, STRIPS, chans), bf16),
            pltpu.VMEM((2 * rows + 4, q + 4, STRIPS, wide), bf16),
            pltpu.VMEM((2 * rows + 2, q + 2, STRIPS, wide), bf16),
            pltpu.VMEM((2, 4, width, 128), f32),
            pltpu.SemaphoreType.DMA((3,)),
        ],
        compiler_params=pltpu.CompilerParams(vmem_limit_bytes=60000 * 1024),
    )(latent, beside, above, below, gain_one.reshape(1, chans), gain_two.reshape(1, chans),
      up_weight, conv_one, conv_two)


def solution(mesh):
    return jax.shard_map(
        functools.partial(local, mesh.shape["ha"]),
        mesh=mesh,
        in_specs=(P("grp", "ha", None, "col"), P(), P(), P(), P(), P()),
        out_specs=P("grp", "ha", "col", None),
        check_vma=False,
    )
```

```python
import functools

import jax
import jax.numpy as jnp
from jax import lax
from jax.experimental import pallas as pl
from jax.experimental.pallas import tpu as pltpu
from jax.sharding import PartitionSpec as P

f32 = jnp.float32
bf16 = jnp.bfloat16
MESH = pl.DeviceIdType.MESH
STRIPS = 16
phase_taps = (((0, 1), (-1, 3)), ((0, 2), (1, 0)))


def exchange_kernel(ha_count, lat, beside, above, below, send, recv):
    ha = lax.axis_index("ha")
    col = lax.axis_index("col")
    rows = lat.shape[1]
    other = {"col": 1 - col}
    has_above, has_below = ha > 0, ha < ha_count - 1

    barrier = pltpu.get_barrier_semaphore()
    pl.semaphore_signal(barrier, 1, device_id=other, device_id_type=MESH)

    @pl.when(has_above)
    def _():
        pl.semaphore_signal(barrier, 1, device_id={"ha": ha - 1}, device_id_type=MESH)

    @pl.when(has_below)
    def _():
        pl.semaphore_signal(barrier, 1, device_id={"ha": ha + 1}, device_id_type=MESH)

    peers = 1 + jnp.minimum(ha, 1) + jnp.minimum(ha_count - 1 - ha, 1)
    pl.semaphore_wait(barrier, peers)

    def copy(src, dst, target, n):
        return pltpu.make_async_remote_copy(
            src_ref=src, dst_ref=dst, send_sem=send.at[n], recv_sem=recv.at[n],
            device_id=target, device_id_type=MESH,
        )

    side = copy(lat.at[0], beside, other, 0)
    down = copy(lat.at[0, pl.ds(rows - 2, 2)], above.at[col], {"ha": ha + 1}, 1)
    up = copy(lat.at[0, pl.ds(0, 2)], below.at[col], {"ha": ha - 1}, 2)
    pass_above = copy(above.at[col], above.at[col], other, 3)
    pass_below = copy(below.at[col], below.at[col], other, 4)

    @pl.when(has_below)
    def _():
        down.start()

    @pl.when(has_above)
    def _():
        up.start()

    side.start()

    @pl.when(has_above)
    def _():
        down.wait_recv()
        pass_above.start()

    @pl.when(has_below)
    def _():
        up.wait_recv()
        pass_below.start()

    side.wait()

    @pl.when(has_above)
    def _():
        up.wait_send()
        pass_above.wait()

    @pl.when(has_below)
    def _():
        down.wait_send()
        pass_below.wait()


def activate(wide, half_gain):
    stats = jnp.sum(wide * wide, axis=-1, keepdims=True) * (1.0 / wide.shape[-1])
    half = wide * lax.rsqrt(stats + 1e-06) * half_gain
    return (half * jnp.tanh(half) + half).astype(bf16)


def block_kernel(
    ha_count, lat, beside, above, below, gain_one, gain_two, up_hbm, one_hbm, two_hbm, out,
    up_w, one_w, two_w, field, strips, ups, first, second, sem
):
    ha = lax.axis_index("ha")
    col = lax.axis_index("col")
    share = lat.shape[2]
    chans = out.shape[2]
    rows, width = lat.shape[1], lat.shape[3]
    half = width // 2
    ql = half // STRIPS
    q = 2 * ql
    depth = 2 * share
    wide = first.shape[3]
    mine = pl.ds(pl.multiple_of(col * share, share), share)
    far = pl.ds(pl.multiple_of((1 - col) * share, share), share)

    inputs = [
        pltpu.make_async_copy(lat.at[0], field.at[pl.ds(2, rows), mine], sem.at[3]),
        pltpu.make_async_copy(beside, field.at[pl.ds(2, rows), far], sem.at[4]),
    ]
    for part in range(2):
        there = pl.ds(part * share, share)
        inputs.append(
            pltpu.make_async_copy(above.at[part], field.at[pl.ds(0, 2), there], sem.at[5 + part])
        )
        inputs.append(
            pltpu.make_async_copy(
                below.at[part], field.at[pl.ds(rows + 2, 2), there], sem.at[7 + part]
            )
        )
    copies = []
    for rp in range(2):
        for cp in range(2):
            tap = 0
            for _, ra in phase_taps[rp]:
                for _, cb in phase_taps[cp]:
                    copies.append(pltpu.make_async_copy(
                        up_hbm.at[ra, cb],
                        up_w.at[rp, cp, :, pl.ds(tap * depth, depth)],
                        sem.at[0],
                    ))
                    tap += 1
    for number, (src, dst) in enumerate(((one_hbm, one_w), (two_hbm, two_w))):
        for a in range(3):
            for b in range(3):
                copies.append(pltpu.make_async_copy(
                    src.at[a, b],
                    dst.at[pl.ds((3 * a + b) * wide, chans)],
                    sem.at[1 + number],
                ))
    for item in inputs + copies:
        item.start()

    for w in (one_w, two_w):
        for n in range(9):
            w[pl.ds(n * wide + chans, wide - chans), :] = jnp.zeros((wide - chans, chans), bf16)

    for item in inputs:
        item.wait()

    @pl.when(ha == 0)
    def _():
        field[pl.ds(0, 2)] = jnp.zeros((2, depth, width), bf16)

    @pl.when(ha == ha_count - 1)
    def _():
        field[pl.ds(rows + 2, 2)] = jnp.zeros((2, depth, width), bf16)

    count = (ql + 4) * STRIPS
    cell = lax.broadcasted_iota(jnp.int32, (count, width), 0)
    place = half * col + ql * (cell % STRIPS) + cell // STRIPS - 2
    pick = (place == lax.broadcasted_iota(jnp.int32, (count, width), 1)).astype(f32).astype(bf16)

    def pick_row(i, carry):
        chosen = lax.dot_general(
            pick, field[i], (((1,), (1,)), ((), ())), preferred_element_type=f32
        )
        strips[i] = chosen.astype(bf16).reshape(ql + 4, STRIPS, depth)
        return carry

    lax.fori_loop(0, rows + 4, pick_row, 0)

    first[:, :, :, pl.ds(chans, wide - chans)] = jnp.zeros(
        first.shape[:3] + (wide - chans,), bf16
    )
    second[:, :, :, pl.ds(chans, wide - chans)] = jnp.zeros(
        second.shape[:3] + (wide - chans,), bf16
    )
    half_one = gain_one[...] * 0.5
    half_two = gain_two[...] * 0.5

    for item in copies[:16]:
        item.wait()

    block = 5
    nt = ql + 2
    for rp in range(2):
        for cp in range(2):
            def up_body(n, carry, rp=rp, cp=cp):
                pieces = []
                for dr, _ in phase_taps[rp]:
                    for dc, _ in phase_taps[cp]:
                        pieces.append(
                            strips[pl.ds(n * block + 1 + dr, block), pl.ds(1 + dc, nt)].reshape(
                                block * nt * STRIPS, depth
                            )
                        )
                lhs = jnp.concatenate(pieces, axis=-1)
                result = lax.dot_general(
                    lhs, up_w[rp, cp], (((1,), (1,)), ((), ())), preferred_element_type=f32
                ).astype(bf16)
                act = activate(result.astype(f32), half_one)
                result = result.reshape(block, nt, STRIPS, chans)
                act = act.reshape(block, nt, STRIPS, chans)
                for u in range(block):
                    for t in range(nt):
                        r = 2 * (n * block + u) + rp
                        ups[r, 2 * t + cp] = result[u, t]
                        first[r, 2 * t + cp, :, pl.ds(0, chans)] = act[u, t]
                return carry

            lax.fori_loop(0, (rows + 2) // block, up_body, 0)

    strip = lax.broadcasted_iota(jnp.int32, (STRIPS, wide), 0)
    low = (strip == 0) & (col == 0)
    high = (strip == STRIPS - 1) & (col == 1)

    def clear(ref, rim):
        count, cols = ref.shape[0], ref.shape[1]

        def clear_row(r, carry):
            for t in range(rim):
                ref[r, t] = jnp.where(low, 0.0, ref[r, t].astype(f32)).astype(bf16)
                e = cols - rim + t
                ref[r, e] = jnp.where(high, 0.0, ref[r, e].astype(f32)).astype(bf16)
            return carry

        lax.fori_loop(0, count, clear_row, 0)

        @pl.when(ha == 0)
        def _():
            ref[pl.ds(0, rim)] = jnp.zeros((rim,) + ref.shape[1:], bf16)

        @pl.when(ha == ha_count - 1)
        def _():
            ref[pl.ds(count - rim, rim)] = jnp.zeros((rim,) + ref.shape[1:], bf16)

    clear(first, 2)

    def windows(ref, start, count, cols):
        return jnp.concatenate(
            [
                ref[pl.ds(start + a, count), pl.ds(b, cols)].reshape(count * cols * STRIPS, wide)
                for a in range(3)
                for b in range(3)
            ],
            axis=-1,
        )

    for item in copies[16:25]:
        item.wait()

    def one_body(n, carry):
        count = 3
        lhs = windows(first, n * count, count, q + 2)
        hidden = jnp.dot(lhs, one_w[...], preferred_element_type=f32).astype(bf16)
        act = activate(hidden.astype(f32), half_two)
        second[pl.ds(n * count, count), :, :, pl.ds(0, chans)] = act.reshape(
            count, q + 2, STRIPS, chans
        )
        return carry

    lax.fori_loop(0, (2 * rows + 2) // 3, one_body, 0)
    clear(second, 1)

    for item in copies[25:]:
        item.wait()

    cell = lax.broadcasted_iota(jnp.int32, (q * STRIPS, width), 0)
    place = q * (cell % STRIPS) + cell // STRIPS
    put = (place == lax.broadcasted_iota(jnp.int32, (q * STRIPS, width), 1)).astype(f32).astype(bf16)

    def two_body(n, carry):
        count = 4
        lhs = windows(second, n * count, count, q)
        total = jnp.dot(lhs, two_w[...], preferred_element_type=f32)
        total = total.reshape(count, q * STRIPS, chans)
        for u in range(count):
            r = n * count + u
            skip = ups[r + 2, pl.ds(2, q)].reshape(q * STRIPS, chans).astype(f32)
            value = (total[u] + skip).astype(bf16)
            out[0, r] = lax.dot_general(
                value, put, (((0,), (0,)), ((), ())), preferred_element_type=f32
            ).astype(bf16)
        return carry

    lax.fori_loop(0, 2 * rows // 4, two_body, 0)


def local(ha_count, latent, up_weight, conv_one, gain_one, conv_two, gain_two):
    _, rows, width, share = latent.shape
    chans = conv_one.shape[3]
    wide = -(-chans // 256) * 256
    ql = width // 2 // STRIPS
    q = 2 * ql
    latent = jnp.transpose(latent, (0, 1, 3, 2))
    up_weight = jnp.transpose(up_weight, (0, 1, 3, 2))
    shapes = [(rows, share, width), (2, 2, share, width), (2, 2, share, width)]
    anywhere = pl.BlockSpec(memory_space=pl.ANY)
    beside, above, below = pl.pallas_call(
        functools.partial(exchange_kernel, ha_count),
        out_shape=[jax.ShapeDtypeStruct(s, bf16) for s in shapes],
        in_specs=[anywhere],
        out_specs=[anywhere] * 3,
        scratch_shapes=[pltpu.SemaphoreType.DMA((5,)), pltpu.SemaphoreType.DMA((5,))],
        compiler_params=pltpu.CompilerParams(collective_id=0, has_side_effects=True),
    )(latent)
    vmem = pl.BlockSpec(memory_space=pltpu.VMEM)
    result = pl.pallas_call(
        functools.partial(block_kernel, ha_count),
        out_shape=jax.ShapeDtypeStruct((1, 2 * rows, chans, width), bf16),
        in_specs=[anywhere] * 4 + [vmem] * 2 + [anywhere] * 3,
        out_specs=vmem,
        scratch_shapes=[
            pltpu.VMEM((2, 2, chans, 8 * share), bf16),
            pltpu.VMEM((9 * wide, chans), bf16),
            pltpu.VMEM((9 * wide, chans), bf16),
            pltpu.VMEM((rows + 4, 2 * share, width), bf16),
            pltpu.VMEM((rows + 4, ql + 4, STRIPS, 2 * share), bf16),
            pltpu.VMEM((2 * rows + 4, q + 4, STRIPS, chans), bf16),
            pltpu.VMEM((2 * rows + 4, q + 4, STRIPS, wide), bf16),
            pltpu.VMEM((2 * rows + 2, q + 2, STRIPS, wide), bf16),
            pltpu.SemaphoreType.DMA((9,)),
        ],
        compiler_params=pltpu.CompilerParams(vmem_limit_bytes=60000 * 1024),
    )(latent, beside, above, below, gain_one.reshape(1, chans), gain_two.reshape(1, chans),
      up_weight, conv_one, conv_two)
    return jnp.transpose(result, (0, 1, 3, 2))


def solution(mesh):
    return jax.shard_map(
        functools.partial(local, mesh.shape["ha"]),
        mesh=mesh,
        in_specs=(P("grp", "ha", None, "col"), P(), P(), P(), P(), P()),
        out_specs=P("grp", "ha", "col", None),
        check_vma=False,
    )
```

```python
import functools

import jax
import jax.numpy as jnp
from jax import lax
from jax.experimental import pallas as pl
from jax.experimental.pallas import tpu as pltpu
from jax.sharding import PartitionSpec as P

f32 = jnp.float32
bf16 = jnp.bfloat16
MESH = pl.DeviceIdType.MESH
STRIPS = 16
phase_taps = (((0, 1), (-1, 3)), ((0, 2), (1, 0)))


def activate(wide, half_gain):
    stats = jnp.sum(wide * wide, axis=-1, keepdims=True) * (1.0 / wide.shape[-1])
    half = wide * lax.rsqrt(stats + 1e-06) * half_gain
    return (half * jnp.tanh(half) + half).astype(bf16)


def block_kernel(
    ha_count, lat, gain_one, gain_two, up_hbm, one_hbm, two_hbm, out,
    up_w, one_w, two_w, field, strips, ups, first, second, sem, send, recv
):
    ha = lax.axis_index("ha")
    col = lax.axis_index("col")
    share = lat.shape[2]
    chans = out.shape[2]
    rows, width = lat.shape[1], lat.shape[3]
    half = width // 2
    ql = half // STRIPS
    q = 2 * ql
    depth = 2 * share
    wide = first.shape[3]
    mine = pl.ds(pl.multiple_of(col * share, share), share)
    other = {"col": 1 - col}
    has_above, has_below = ha > 0, ha < ha_count - 1

    barrier = pltpu.get_barrier_semaphore()
    pl.semaphore_signal(barrier, 1, device_id=other, device_id_type=MESH)

    @pl.when(has_above)
    def _():
        pl.semaphore_signal(barrier, 1, device_id={"ha": ha - 1}, device_id_type=MESH)

    @pl.when(has_below)
    def _():
        pl.semaphore_signal(barrier, 1, device_id={"ha": ha + 1}, device_id_type=MESH)

    own = pltpu.make_async_copy(lat.at[0], field.at[pl.ds(2, rows), mine], sem.at[3])
    own.start()

    copies = []
    for rp in range(2):
        for cp in range(2):
            tap = 0
            for _, ra in phase_taps[rp]:
                for _, cb in phase_taps[cp]:
                    copies.append(pltpu.make_async_copy(
                        up_hbm.at[ra, cb],
                        up_w.at[rp, cp, :, pl.ds(tap * depth, depth)],
                        sem.at[0],
                    ))
                    tap += 1
    for number, (src, dst) in enumerate(((one_hbm, one_w), (two_hbm, two_w))):
        for a in range(3):
            for b in range(3):
                copies.append(pltpu.make_async_copy(
                    src.at[a, b],
                    dst.at[pl.ds((3 * a + b) * wide, chans)],
                    sem.at[1 + number],
                ))
    for item in copies:
        item.start()

    peers = 1 + jnp.minimum(ha, 1) + jnp.minimum(ha_count - 1 - ha, 1)
    pl.semaphore_wait(barrier, peers)

    def remote(src, dst, target, n):
        return pltpu.make_async_remote_copy(
            src_ref=src, dst_ref=dst, send_sem=send.at[n], recv_sem=recv.at[n],
            device_id=target, device_id_type=MESH,
        )

    top, bottom = field.at[pl.ds(0, 2), mine], field.at[pl.ds(rows + 2, 2), mine]
    side = remote(lat.at[0], field.at[pl.ds(2, rows), mine], other, 0)
    down = remote(lat.at[0, pl.ds(rows - 2, 2)], top, {"ha": ha + 1}, 1)
    up = remote(lat.at[0, pl.ds(0, 2)], bottom, {"ha": ha - 1}, 2)
    pass_top = remote(top, top, other, 3)
    pass_bottom = remote(bottom, bottom, other, 4)

    @pl.when(has_below)
    def _():
        down.start()

    @pl.when(has_above)
    def _():
        up.start()

    side.start()

    for w in (one_w, two_w):
        for n in range(9):
            w[pl.ds(n * wide + chans, wide - chans), :] = jnp.zeros((wide - chans, chans), bf16)

    @pl.when(ha == 0)
    def _():
        field[pl.ds(0, 2)] = jnp.zeros((2, depth, width), bf16)

    @pl.when(ha == ha_count - 1)
    def _():
        field[pl.ds(rows + 2, 2)] = jnp.zeros((2, depth, width), bf16)

    first[:, :, :, pl.ds(chans, wide - chans)] = jnp.zeros(
        first.shape[:3] + (wide - chans,), bf16
    )
    second[:, :, :, pl.ds(chans, wide - chans)] = jnp.zeros(
        second.shape[:3] + (wide - chans,), bf16
    )
    count = (ql + 4) * STRIPS
    cell = lax.broadcasted_iota(jnp.int32, (count, width), 0)
    place = half * col + ql * (cell % STRIPS) + cell // STRIPS - 2
    pick = (place == lax.broadcasted_iota(jnp.int32, (count, width), 1)).astype(f32).astype(bf16)

    def pick_row(i, carry):
        chosen = lax.dot_general(
            pick, field[i], (((1,), (1,)), ((), ())), preferred_element_type=f32
        )
        strips[i] = chosen.astype(bf16).reshape(ql + 4, STRIPS, depth)
        return carry

    own.wait()
    side.wait()
    lax.fori_loop(2, rows + 2, pick_row, 0)

    half_one = gain_one[...] * 0.5
    half_two = gain_two[...] * 0.5

    for item in copies[:16]:
        item.wait()

    nt = ql + 2

    def upsample(groups, rp, cp):
        pieces = []
        for dr, _ in phase_taps[rp]:
            for dc, _ in phase_taps[cp]:
                parts = [
                    strips[pl.ds(start + 1 + dr, n), pl.ds(1 + dc, nt)].reshape(
                        n * nt * STRIPS, depth
                    )
                    for start, n in groups
                ]
                pieces.append(parts[0] if len(parts) == 1 else jnp.concatenate(parts, axis=0))
        lhs = jnp.concatenate(pieces, axis=-1)
        result = lax.dot_general(
            lhs, up_w[rp, cp], (((1,), (1,)), ((), ())), preferred_element_type=f32
        ).astype(bf16)
        act = activate(result.astype(f32), half_one)
        targets = [start + u for start, n in groups for u in range(n)]
        result = result.reshape(len(targets), nt, STRIPS, chans)
        act = act.reshape(len(targets), nt, STRIPS, chans)
        for u, target in enumerate(targets):
            for t in range(nt):
                ups[2 * target + rp, 2 * t + cp] = result[u, t]
                first[2 * target + rp, 2 * t + cp, :, pl.ds(0, chans)] = act[u, t]

    inner = ((2, rows - 2),)
    outer = ((0, 2), (rows, 2))
    upsample(inner, 0, 0)
    upsample(inner, 0, 1)

    @pl.when(has_above)
    def _():
        down.wait_recv()
        pass_top.start()

    @pl.when(has_below)
    def _():
        up.wait_recv()
        pass_bottom.start()

    upsample(inner, 1, 0)
    upsample(inner, 1, 1)

    @pl.when(has_above)
    def _():
        up.wait_send()
        pass_top.wait()

    @pl.when(has_below)
    def _():
        down.wait_send()
        pass_bottom.wait()

    lax.fori_loop(0, 2, pick_row, 0)
    lax.fori_loop(rows + 2, rows + 4, pick_row, 0)
    for rp in range(2):
        for cp in range(2):
            upsample(outer, rp, cp)

    strip = lax.broadcasted_iota(jnp.int32, (STRIPS, wide), 0)
    low = (strip == 0) & (col == 0)
    high = (strip == STRIPS - 1) & (col == 1)

    def clear(ref, rim):
        count, cols = ref.shape[0], ref.shape[1]

        def clear_row(r, carry):
            for t in range(rim):
                ref[r, t] = jnp.where(low, 0.0, ref[r, t].astype(f32)).astype(bf16)
                e = cols - rim + t
                ref[r, e] = jnp.where(high, 0.0, ref[r, e].astype(f32)).astype(bf16)
            return carry

        lax.fori_loop(0, count, clear_row, 0)

        @pl.when(ha == 0)
        def _():
            ref[pl.ds(0, rim)] = jnp.zeros((rim,) + ref.shape[1:], bf16)

        @pl.when(ha == ha_count - 1)
        def _():
            ref[pl.ds(count - rim, rim)] = jnp.zeros((rim,) + ref.shape[1:], bf16)

    clear(first, 2)

    def windows(ref, start, count, cols):
        return jnp.concatenate(
            [
                ref[pl.ds(start + a, count), pl.ds(b, cols)].reshape(count * cols * STRIPS, wide)
                for a in range(3)
                for b in range(3)
            ],
            axis=-1,
        )

    for item in copies[16:25]:
        item.wait()

    def one_body(n, carry):
        count = 3
        lhs = windows(first, n * count, count, q + 2)
        hidden = jnp.dot(lhs, one_w[...], preferred_element_type=f32).astype(bf16)
        act = activate(hidden.astype(f32), half_two)
        second[pl.ds(n * count, count), :, :, pl.ds(0, chans)] = act.reshape(
            count, q + 2, STRIPS, chans
        )
        return carry

    lax.fori_loop(0, (2 * rows + 2) // 3, one_body, 0)
    clear(second, 1)

    for item in copies[25:]:
        item.wait()

    cell = lax.broadcasted_iota(jnp.int32, (q * STRIPS, width), 0)
    place = q * (cell % STRIPS) + cell // STRIPS
    put = (place == lax.broadcasted_iota(jnp.int32, (q * STRIPS, width), 1)).astype(f32).astype(bf16)

    def two_body(n, carry):
        count = 4
        lhs = windows(second, n * count, count, q)
        total = jnp.dot(lhs, two_w[...], preferred_element_type=f32)
        total = total.reshape(count, q * STRIPS, chans)
        for u in range(count):
            r = n * count + u
            skip = ups[r + 2, pl.ds(2, q)].reshape(q * STRIPS, chans).astype(f32)
            value = (total[u] + skip).astype(bf16)
            out[0, r] = lax.dot_general(
                value, put, (((0,), (0,)), ((), ())), preferred_element_type=f32
            ).astype(bf16)
        return carry

    lax.fori_loop(0, 2 * rows // 4, two_body, 0)


def local(ha_count, latent, up_weight, conv_one, gain_one, conv_two, gain_two):
    _, rows, width, share = latent.shape
    chans = conv_one.shape[3]
    wide = -(-chans // 256) * 256
    ql = width // 2 // STRIPS
    q = 2 * ql
    latent = jnp.transpose(latent, (0, 1, 3, 2))
    up_weight = jnp.transpose(up_weight, (0, 1, 3, 2))
    anywhere = pl.BlockSpec(memory_space=pl.ANY)
    vmem = pl.BlockSpec(memory_space=pltpu.VMEM)
    result = pl.pallas_call(
        functools.partial(block_kernel, ha_count),
        out_shape=jax.ShapeDtypeStruct((1, 2 * rows, chans, width), bf16),
        in_specs=[anywhere] + [vmem] * 2 + [anywhere] * 3,
        out_specs=vmem,
        scratch_shapes=[
            pltpu.VMEM((2, 2, chans, 8 * share), bf16),
            pltpu.VMEM((9 * wide, chans), bf16),
            pltpu.VMEM((9 * wide, chans), bf16),
            pltpu.VMEM((rows + 4, 2 * share, width), bf16),
            pltpu.VMEM((rows + 4, ql + 4, STRIPS, 2 * share), bf16),
            pltpu.VMEM((2 * rows + 4, q + 4, STRIPS, chans), bf16),
            pltpu.VMEM((2 * rows + 4, q + 4, STRIPS, wide), bf16),
            pltpu.VMEM((2 * rows + 2, q + 2, STRIPS, wide), bf16),
            pltpu.SemaphoreType.DMA((4,)),
            pltpu.SemaphoreType.DMA((5,)),
            pltpu.SemaphoreType.DMA((5,)),
        ],
        compiler_params=pltpu.CompilerParams(
            vmem_limit_bytes=60000 * 1024, collective_id=0, has_side_effects=True
        ),
    )(latent, gain_one.reshape(1, chans), gain_two.reshape(1, chans),
      up_weight, conv_one, conv_two)
    return jnp.transpose(result, (0, 1, 3, 2))


def solution(mesh):
    return jax.shard_map(
        functools.partial(local, mesh.shape["ha"]),
        mesh=mesh,
        in_specs=(P("grp", "ha", None, "col"), P(), P(), P(), P(), P()),
        out_specs=P("grp", "ha", "col", None),
        check_vma=False,
    )
```

```python
import functools

import jax
import jax.numpy as jnp
from jax import lax
from jax.experimental import pallas as pl
from jax.experimental.pallas import tpu as pltpu
from jax.sharding import PartitionSpec as P

f32 = jnp.float32
bf16 = jnp.bfloat16
MESH = pl.DeviceIdType.MESH
STRIPS = 16
phase_taps = (((0, 1), (-1, 3)), ((0, 2), (1, 0)))


def activate(wide, half_gain):
    stats = jnp.sum(wide * wide, axis=-1, keepdims=True) * (1.0 / wide.shape[-1])
    half = wide * lax.rsqrt(stats + 1e-06) * half_gain
    return half * jnp.tanh(half) + half


def block_kernel(
    ha_count, lat, gain_one, gain_two, up_hbm, one_hbm, two_hbm, out,
    up_w, one_w, two_w, field, strips, ups, first, second, sem, send, recv
):
    ha = lax.axis_index("ha")
    col = lax.axis_index("col")
    share = lat.shape[2]
    chans = out.shape[2]
    rows, width = lat.shape[1], lat.shape[3]
    half = width // 2
    ql = half // STRIPS
    q = 2 * ql
    depth = 2 * share
    lead = 128
    tail = chans - lead
    mine = pl.ds(pl.multiple_of(col * share, share), share)
    other = {"col": 1 - col}
    has_above, has_below = ha > 0, ha < ha_count - 1

    barrier = pltpu.get_barrier_semaphore()
    pl.semaphore_signal(barrier, 1, device_id=other, device_id_type=MESH)

    @pl.when(has_above)
    def _():
        pl.semaphore_signal(barrier, 1, device_id={"ha": ha - 1}, device_id_type=MESH)

    @pl.when(has_below)
    def _():
        pl.semaphore_signal(barrier, 1, device_id={"ha": ha + 1}, device_id_type=MESH)

    own = pltpu.make_async_copy(lat.at[0], field.at[pl.ds(2, rows), mine], sem.at[3])
    own.start()

    copies = []
    for rp in range(2):
        for cp in range(2):
            tap = 0
            for _, ra in phase_taps[rp]:
                for _, cb in phase_taps[cp]:
                    copies.append(pltpu.make_async_copy(
                        up_hbm.at[ra, cb],
                        up_w.at[rp, cp, :, pl.ds(tap * depth, depth)],
                        sem.at[0],
                    ))
                    tap += 1
    for number, (src, dst) in enumerate(((one_hbm, one_w), (two_hbm, two_w))):
        for a in range(3):
            for b in range(3):
                at = a * 4 * lead + b * lead
                copies.append(pltpu.make_async_copy(
                    src.at[a, b, pl.ds(0, lead)], dst.at[pl.ds(at, lead)], sem.at[1 + number]
                ))
                at = a * 4 * lead + 3 * lead + b * tail if b < 2 else 12 * lead + a * tail
                copies.append(pltpu.make_async_copy(
                    src.at[a, b, pl.ds(lead, tail)], dst.at[pl.ds(at, tail)], sem.at[1 + number]
                ))
    for item in copies:
        item.start()

    peers = 1 + jnp.minimum(ha, 1) + jnp.minimum(ha_count - 1 - ha, 1)
    pl.semaphore_wait(barrier, peers)

    def remote(src, dst, target, n):
        return pltpu.make_async_remote_copy(
            src_ref=src, dst_ref=dst, send_sem=send.at[n], recv_sem=recv.at[n],
            device_id=target, device_id_type=MESH,
        )

    top, bottom = field.at[pl.ds(0, 2), mine], field.at[pl.ds(rows + 2, 2), mine]
    side = remote(lat.at[0], field.at[pl.ds(2, rows), mine], other, 0)
    down = remote(lat.at[0, pl.ds(rows - 2, 2)], top, {"ha": ha + 1}, 1)
    up = remote(lat.at[0, pl.ds(0, 2)], bottom, {"ha": ha - 1}, 2)
    pass_top = remote(top, top, other, 3)
    pass_bottom = remote(bottom, bottom, other, 4)

    @pl.when(has_below)
    def _():
        down.start()

    @pl.when(has_above)
    def _():
        up.start()

    side.start()

    for w in (one_w, two_w):
        w[pl.ds(12 * lead + 3 * tail, 2 * lead - 3 * tail)] = jnp.zeros(
            (2 * lead - 3 * tail, chans), bf16
        )
    for _, _, under in (first, second):
        last = under.shape[0] - 1
        under[last] = jnp.zeros(under.shape[1:], bf16)

    @pl.when(ha == 0)
    def _():
        field[pl.ds(0, 2)] = jnp.zeros((2, depth, width), bf16)

    @pl.when(ha == ha_count - 1)
    def _():
        field[pl.ds(rows + 2, 2)] = jnp.zeros((2, depth, width), bf16)

    strip = lax.broadcasted_iota(jnp.int32, (STRIPS, chans), 0)
    keep_low = (strip > 0) | (col > 0)
    keep_high = (strip < STRIPS - 1) | (col < 1)

    def keep(refs, r, t, value):
        ahead, next_col, next_row = refs
        value = value.astype(bf16)
        rest = value[:, lead:]
        ahead[r, t] = value[:, :lead]
        next_col[r, t + 1, :, pl.ds(0, tail)] = rest
        next_col[r, t, :, pl.ds(tail, tail)] = rest
        next_row[r + 1, t, :, pl.ds(0, tail)] = rest
        next_row[r, t, :, pl.ds(tail, tail)] = rest

    def windows(refs, start, count, cols):
        ahead, next_col, next_row = refs

        def flat(ref, r, t):
            return ref[pl.ds(r, count), pl.ds(t, cols)].reshape(count * cols * STRIPS, lead)

        pieces = []
        for a in range(3):
            pieces += [flat(ahead, start + a, b) for b in range(3)]
            pieces.append(flat(next_col, start + a, 1))
        pieces += [flat(next_row, start + 1, 2), flat(next_row, start + 3, 2)]
        return jnp.concatenate(pieces, axis=-1)

    count = (ql + 4) * STRIPS
    cell = lax.broadcasted_iota(jnp.int32, (count, width), 0)
    place = half * col + ql * (cell % STRIPS) + cell // STRIPS - 2
    pick = (place == lax.broadcasted_iota(jnp.int32, (count, width), 1)).astype(f32).astype(bf16)

    def pick_row(i, carry):
        chosen = lax.dot_general(
            pick, field[i], (((1,), (1,)), ((), ())), preferred_element_type=f32
        )
        strips[i] = chosen.astype(bf16).reshape(ql + 4, STRIPS, depth)
        return carry

    own.wait()
    side.wait()
    lax.fori_loop(2, rows + 2, pick_row, 0, unroll=4)

    half_one = gain_one[...] * 0.5
    half_two = gain_two[...] * 0.5

    for item in copies[:16]:
        item.wait()

    nt = ql + 2

    def upsample(groups, rp, cp):
        pieces = []
        for dr, _ in phase_taps[rp]:
            for dc, _ in phase_taps[cp]:
                parts = [
                    strips[pl.ds(start + 1 + dr, n), pl.ds(1 + dc, nt)].reshape(
                        n * nt * STRIPS, depth
                    )
                    for start, n in groups
                ]
                pieces.append(parts[0] if len(parts) == 1 else jnp.concatenate(parts, axis=0))
        lhs = jnp.concatenate(pieces, axis=-1)
        result = lax.dot_general(
            lhs, up_w[rp, cp], (((1,), (1,)), ((), ())), preferred_element_type=f32
        ).astype(bf16)
        act = activate(result.astype(f32), half_one)
        targets = [start + u for start, n in groups for u in range(n)]
        result = result.reshape(len(targets), nt, STRIPS, chans)
        act = act.reshape(len(targets), nt, STRIPS, chans)
        for u, target in enumerate(targets):
            for t in range(nt):
                value = act[u, t]
                if t == 0:
                    value = jnp.where(keep_low, value, 0.0)
                if t == nt - 1:
                    value = jnp.where(keep_high, value, 0.0)
                if target == 0:
                    value = jnp.where(has_above, value, 0.0)
                if target == rows + 1:
                    value = jnp.where(has_below, value, 0.0)
                ups[2 * target + rp, 2 * t + cp] = result[u, t]
                keep(first, 2 * target + rp, 2 * t + cp, value)

    inner = ((2, rows - 2),)
    outer = ((0, 2), (rows, 2))
    upsample(inner, 0, 0)
    upsample(inner, 0, 1)

    @pl.when(has_above)
    def _():
        down.wait_recv()
        pass_top.start()

    @pl.when(has_below)
    def _():
        up.wait_recv()
        pass_bottom.start()

    upsample(inner, 1, 0)
    upsample(inner, 1, 1)

    @pl.when(has_above)
    def _():
        up.wait_send()
        pass_top.wait()

    @pl.when(has_below)
    def _():
        down.wait_send()
        pass_bottom.wait()

    lax.fori_loop(0, 2, pick_row, 0, unroll=2)
    lax.fori_loop(rows + 2, rows + 4, pick_row, 0, unroll=2)
    for rp in range(2):
        for cp in range(2):
            upsample(outer, rp, cp)

    for item in copies[16:34]:
        item.wait()

    def one_body(n, carry):
        count = 3
        lhs = windows(first, n * count, count, q + 2)
        hidden = jnp.dot(lhs, one_w[...], preferred_element_type=f32).astype(bf16)
        act = activate(hidden.astype(f32), half_two)
        act = act.reshape(count, q + 2, STRIPS, chans)
        for u in range(count):
            for t in range(q + 2):
                value = act[u, t]
                if t == 0:
                    value = jnp.where(keep_low, value, 0.0)
                if t == q + 1:
                    value = jnp.where(keep_high, value, 0.0)
                if u == 0:
                    value = jnp.where((n > 0) | has_above, value, 0.0)
                if u == count - 1:
                    value = jnp.where((n < chunks - 1) | has_below, value, 0.0)
                keep(second, n * count + u, t, value)
        return carry

    chunks = (2 * rows + 2) // 3
    lax.fori_loop(0, chunks, one_body, 0)

    for item in copies[34:]:
        item.wait()

    cell = lax.broadcasted_iota(jnp.int32, (q * STRIPS, width), 0)
    place = q * (cell % STRIPS) + cell // STRIPS
    put = (place == lax.broadcasted_iota(jnp.int32, (q * STRIPS, width), 1)).astype(f32).astype(bf16)

    def two_body(n, carry):
        count = 4
        lhs = windows(second, n * count, count, q)
        total = jnp.dot(lhs, two_w[...], preferred_element_type=f32)
        total = total.reshape(count, q * STRIPS, chans)
        for u in range(count):
            r = n * count + u
            skip = ups[r + 2, pl.ds(2, q)].reshape(q * STRIPS, chans).astype(f32)
            value = (total[u] + skip).astype(bf16)
            out[0, r] = lax.dot_general(
                value, put, (((0,), (0,)), ((), ())), preferred_element_type=f32
            ).astype(bf16)
        return carry

    lax.fori_loop(0, 2 * rows // 4, two_body, 0)


def packed(rows, cols):
    return [
        pltpu.VMEM((rows, cols, STRIPS, 128), bf16),
        pltpu.VMEM((rows, cols + 1, STRIPS, 128), bf16),
        pltpu.VMEM((rows + 1, cols, STRIPS, 128), bf16),
    ]


def local(ha_count, latent, up_weight, conv_one, gain_one, conv_two, gain_two):
    _, rows, width, share = latent.shape
    chans = conv_one.shape[3]
    ql = width // 2 // STRIPS
    q = 2 * ql
    latent = jnp.transpose(latent, (0, 1, 3, 2))
    up_weight = jnp.transpose(up_weight, (0, 1, 3, 2))
    anywhere = pl.BlockSpec(memory_space=pl.ANY)
    vmem = pl.BlockSpec(memory_space=pltpu.VMEM)
    result = pl.pallas_call(
        functools.partial(block_kernel, ha_count),
        out_shape=jax.ShapeDtypeStruct((1, 2 * rows, chans, width), bf16),
        in_specs=[anywhere] + [vmem] * 2 + [anywhere] * 3,
        out_specs=vmem,
        scratch_shapes=[
            pltpu.VMEM((2, 2, chans, 8 * share), bf16),
            pltpu.VMEM((14 * 128, chans), bf16),
            pltpu.VMEM((14 * 128, chans), bf16),
            pltpu.VMEM((rows + 4, 2 * share, width), bf16),
            pltpu.VMEM((rows + 4, ql + 4, STRIPS, 2 * share), bf16),
            pltpu.VMEM((2 * rows + 4, q + 4, STRIPS, chans), bf16),
            packed(2 * rows + 4, q + 4),
            packed(2 * rows + 2, q + 2),
            pltpu.SemaphoreType.DMA((4,)),
            pltpu.SemaphoreType.DMA((5,)),
            pltpu.SemaphoreType.DMA((5,)),
        ],
        compiler_params=pltpu.CompilerParams(
            vmem_limit_bytes=60000 * 1024, collective_id=0, has_side_effects=True
        ),
    )(latent, gain_one.reshape(1, chans), gain_two.reshape(1, chans),
      up_weight, conv_one, conv_two)
    return jnp.transpose(result, (0, 1, 3, 2))


def solution(mesh):
    return jax.shard_map(
        functools.partial(local, mesh.shape["ha"]),
        mesh=mesh,
        in_specs=(P("grp", "ha", None, "col"), P(), P(), P(), P(), P()),
        out_specs=P("grp", "ha", "col", None),
        check_vma=False,
    )
```

```python
import functools

import jax
import jax.numpy as jnp
from jax import lax
from jax.experimental import pallas as pl
from jax.experimental.pallas import tpu as pltpu
from jax.sharding import PartitionSpec as P

f32 = jnp.float32
bf16 = jnp.bfloat16
MESH = pl.DeviceIdType.MESH
STRIPS = 16
phase_taps = (((0, 1), (-1, 3)), ((0, 2), (1, 0)))


def activate(wide, half_gain):
    stats = jnp.sum(wide * wide, axis=-1, keepdims=True) * (1.0 / wide.shape[-1])
    half = wide * lax.rsqrt(stats + 1e-06) * half_gain
    return half * jnp.tanh(half) + half


def block_kernel(
    ha_count, lat, gain_one, gain_two, up_hbm, one_hbm, two_hbm, out,
    up_w, one_w, two_w, field, strips, ups, first, second, sem, send, recv
):
    ha = lax.axis_index("ha")
    col = lax.axis_index("col")
    share = lat.shape[2]
    chans = out.shape[2]
    rows, width = lat.shape[1], lat.shape[3]
    half = width // 2
    ql = half // STRIPS
    q = 2 * ql
    depth = 2 * share
    lead = 128
    tail = chans - lead
    mine = pl.ds(pl.multiple_of(col * share, share), share)
    other = {"col": 1 - col}
    has_above, has_below = ha > 0, ha < ha_count - 1

    barrier = pltpu.get_barrier_semaphore()
    pl.semaphore_signal(barrier, 1, device_id=other, device_id_type=MESH)

    @pl.when(has_above)
    def _():
        pl.semaphore_signal(barrier, 1, device_id={"ha": ha - 1}, device_id_type=MESH)

    @pl.when(has_below)
    def _():
        pl.semaphore_signal(barrier, 1, device_id={"ha": ha + 1}, device_id_type=MESH)

    own = pltpu.make_async_copy(lat.at[0], field.at[pl.ds(2, rows), mine], sem.at[3])
    own.start()

    copies = []
    for rp in range(2):
        for cp in range(2):
            tap = 0
            for _, ra in phase_taps[rp]:
                for _, cb in phase_taps[cp]:
                    copies.append(pltpu.make_async_copy(
                        up_hbm.at[ra, cb],
                        up_w.at[rp, cp, :, pl.ds(tap * depth, depth)],
                        sem.at[0],
                    ))
                    tap += 1
    for number, (src, dst) in enumerate(((one_hbm, one_w), (two_hbm, two_w))):
        for a in range(3):
            for b in range(3):
                at = a * 4 * lead + b * lead
                copies.append(pltpu.make_async_copy(
                    src.at[a, b, pl.ds(0, lead)], dst.at[pl.ds(at, lead)], sem.at[1 + number]
                ))
                at = a * 4 * lead + 3 * lead + b * tail if b < 2 else 12 * lead + a * tail
                copies.append(pltpu.make_async_copy(
                    src.at[a, b, pl.ds(lead, tail)], dst.at[pl.ds(at, tail)], sem.at[1 + number]
                ))
    for item in copies:
        item.start()

    peers = 1 + jnp.minimum(ha, 1) + jnp.minimum(ha_count - 1 - ha, 1)
    pl.semaphore_wait(barrier, peers)

    def remote(src, dst, target, n):
        return pltpu.make_async_remote_copy(
            src_ref=src, dst_ref=dst, send_sem=send.at[n], recv_sem=recv.at[n],
            device_id=target, device_id_type=MESH,
        )

    top, bottom = field.at[pl.ds(0, 2), mine], field.at[pl.ds(rows + 2, 2), mine]
    side = remote(lat.at[0], field.at[pl.ds(2, rows), mine], other, 0)
    down = remote(lat.at[0, pl.ds(rows - 2, 2)], top, {"ha": ha + 1}, 1)
    up = remote(lat.at[0, pl.ds(0, 2)], bottom, {"ha": ha - 1}, 2)
    pass_top = remote(top, top, other, 3)
    pass_bottom = remote(bottom, bottom, other, 4)

    @pl.when(has_below)
    def _():
        down.start()

    @pl.when(has_above)
    def _():
        up.start()

    side.start()

    for w in (one_w, two_w):
        w[pl.ds(12 * lead + 3 * tail, 2 * lead - 3 * tail)] = jnp.zeros(
            (2 * lead - 3 * tail, chans), bf16
        )
    for _, _, under in (first, second):
        last = under.shape[0] - 1
        under[last] = jnp.zeros(under.shape[1:], bf16)

    @pl.when(ha == 0)
    def _():
        field[pl.ds(0, 2)] = jnp.zeros((2, depth, width), bf16)

    @pl.when(ha == ha_count - 1)
    def _():
        field[pl.ds(rows + 2, 2)] = jnp.zeros((2, depth, width), bf16)

    strip = lax.broadcasted_iota(jnp.int32, (STRIPS, chans), 0)
    keep_low = (strip > 0) | (col > 0)
    keep_high = (strip < STRIPS - 1) | (col < 1)

    def keep(refs, r, t, value):
        ahead, next_col, next_row = refs
        value = value.astype(bf16)
        rest = value[:, lead:]
        ahead[r, t] = value[:, :lead]
        next_col[r, t + 1, :, pl.ds(0, tail)] = rest
        next_col[r, t, :, pl.ds(tail, tail)] = rest
        next_row[r + 1, t, :, pl.ds(0, tail)] = rest
        next_row[r, t, :, pl.ds(tail, tail)] = rest

    def windows(refs, start, count, cols):
        ahead, next_col, next_row = refs

        def flat(ref, r, t):
            return ref[pl.ds(r, count), pl.ds(t, cols)].reshape(count * cols * STRIPS, lead)

        pieces = []
        for a in range(3):
            pieces += [flat(ahead, start + a, b) for b in range(3)]
            pieces.append(flat(next_col, start + a, 1))
        pieces += [flat(next_row, start + 1, 2), flat(next_row, start + 3, 2)]
        return jnp.concatenate(pieces, axis=-1)

    count = (ql + 4) * STRIPS
    cell = lax.broadcasted_iota(jnp.int32, (count, width), 0)
    place = half * col + ql * (cell % STRIPS) + cell // STRIPS - 2
    pick = (place == lax.broadcasted_iota(jnp.int32, (count, width), 1)).astype(f32).astype(bf16)

    def pick_row(i, carry):
        chosen = lax.dot_general(
            pick, field[i], (((1,), (1,)), ((), ())), preferred_element_type=f32
        )
        strips[i] = chosen.astype(bf16).reshape(ql + 4, STRIPS, depth)
        return carry

    own.wait()
    side.wait()
    lax.fori_loop(2, rows + 2, pick_row, 0, unroll=4)

    half_one = gain_one[...] * 0.5
    half_two = gain_two[...] * 0.5

    for item in copies[:16]:
        item.wait()

    nt = ql + 2

    def upsample(groups, rp, cp):
        pieces = []
        for dr, _ in phase_taps[rp]:
            for dc, _ in phase_taps[cp]:
                parts = [
                    strips[pl.ds(start + 1 + dr, n), pl.ds(1 + dc, nt)].reshape(
                        n * nt * STRIPS, depth
                    )
                    for start, n in groups
                ]
                pieces.append(parts[0] if len(parts) == 1 else jnp.concatenate(parts, axis=0))
        lhs = jnp.concatenate(pieces, axis=-1)
        result = lax.dot_general(
            lhs, up_w[rp, cp], (((1,), (1,)), ((), ())), preferred_element_type=f32
        ).astype(bf16)
        act = activate(result.astype(f32), half_one)
        targets = [start + u for start, n in groups for u in range(n)]
        result = result.reshape(len(targets), nt, STRIPS, chans)
        act = act.reshape(len(targets), nt, STRIPS, chans)
        for u, target in enumerate(targets):
            for t in range(nt):
                value = act[u, t]
                if t == 0:
                    value = jnp.where(keep_low, value, 0.0)
                if t == nt - 1:
                    value = jnp.where(keep_high, value, 0.0)
                if target == 0:
                    value = jnp.where(has_above, value, 0.0)
                if target == rows + 1:
                    value = jnp.where(has_below, value, 0.0)
                ups[2 * target + rp, 2 * t + cp] = result[u, t]
                keep(first, 2 * target + rp, 2 * t + cp, value)

    inner = ((2, rows - 2),)
    outer = ((0, 2), (rows, 2))
    upsample(inner, 0, 0)
    upsample(inner, 0, 1)

    @pl.when(has_above)
    def _():
        down.wait_recv()
        pass_top.start()

    @pl.when(has_below)
    def _():
        up.wait_recv()
        pass_bottom.start()

    upsample(inner, 1, 0)
    upsample(inner, 1, 1)

    @pl.when(has_above)
    def _():
        up.wait_send()
        pass_top.wait()

    @pl.when(has_below)
    def _():
        down.wait_send()
        pass_bottom.wait()

    lax.fori_loop(0, 2, pick_row, 0, unroll=2)
    lax.fori_loop(rows + 2, rows + 4, pick_row, 0, unroll=2)
    for rp in range(2):
        for cp in range(2):
            upsample(outer, rp, cp)

    for item in copies[16:34]:
        item.wait()

    def one_body(n, carry):
        count = 3
        lhs = windows(first, n * count, count, q + 2)
        hidden = jnp.dot(lhs, one_w[...], preferred_element_type=f32).astype(bf16)
        act = activate(hidden.astype(f32), half_two)
        act = act.reshape(count, q + 2, STRIPS, chans)
        for u in range(count):
            for t in range(q + 2):
                value = act[u, t]
                if t == 0:
                    value = jnp.where(keep_low, value, 0.0)
                if t == q + 1:
                    value = jnp.where(keep_high, value, 0.0)
                if u == 0:
                    value = jnp.where((n > 0) | has_above, value, 0.0)
                if u == count - 1:
                    value = jnp.where((n < chunks - 1) | has_below, value, 0.0)
                keep(second, n * count + u, t, value)
        return carry

    chunks = (2 * rows + 2) // 3
    lax.fori_loop(0, chunks, one_body, 0, unroll=2)

    for item in copies[34:]:
        item.wait()

    cell = lax.broadcasted_iota(jnp.int32, (q * STRIPS, width), 0)
    place = q * (cell % STRIPS) + cell // STRIPS
    put = (place == lax.broadcasted_iota(jnp.int32, (q * STRIPS, width), 1)).astype(f32).astype(bf16)

    def two_body(n, carry):
        count = 4
        lhs = windows(second, n * count, count, q)
        total = jnp.dot(lhs, two_w[...], preferred_element_type=f32)
        total = total.reshape(count, q * STRIPS, chans)
        for u in range(count):
            r = n * count + u
            skip = ups[r + 2, pl.ds(2, q)].reshape(q * STRIPS, chans).astype(f32)
            value = (total[u] + skip).astype(bf16)
            out[0, r] = lax.dot_general(
                value, put, (((0,), (0,)), ((), ())), preferred_element_type=f32
            ).astype(bf16)
        return carry

    lax.fori_loop(0, 2 * rows // 4, two_body, 0, unroll=2)


def packed(rows, cols):
    return [
        pltpu.VMEM((rows, cols, STRIPS, 128), bf16),
        pltpu.VMEM((rows, cols + 1, STRIPS, 128), bf16),
        pltpu.VMEM((rows + 1, cols, STRIPS, 128), bf16),
    ]


def local(ha_count, latent, up_weight, conv_one, gain_one, conv_two, gain_two):
    _, rows, width, share = latent.shape
    chans = conv_one.shape[3]
    ql = width // 2 // STRIPS
    q = 2 * ql
    latent = jnp.transpose(latent, (0, 1, 3, 2))
    up_weight = jnp.transpose(up_weight, (0, 1, 3, 2))
    anywhere = pl.BlockSpec(memory_space=pl.ANY)
    vmem = pl.BlockSpec(memory_space=pltpu.VMEM)
    result = pl.pallas_call(
        functools.partial(block_kernel, ha_count),
        out_shape=jax.ShapeDtypeStruct((1, 2 * rows, chans, width), bf16),
        in_specs=[anywhere] + [vmem] * 2 + [anywhere] * 3,
        out_specs=vmem,
        scratch_shapes=[
            pltpu.VMEM((2, 2, chans, 8 * share), bf16),
            pltpu.VMEM((14 * 128, chans), bf16),
            pltpu.VMEM((14 * 128, chans), bf16),
            pltpu.VMEM((rows + 4, 2 * share, width), bf16),
            pltpu.VMEM((rows + 4, ql + 4, STRIPS, 2 * share), bf16),
            pltpu.VMEM((2 * rows + 4, q + 4, STRIPS, chans), bf16),
            packed(2 * rows + 4, q + 4),
            packed(2 * rows + 2, q + 2),
            pltpu.SemaphoreType.DMA((4,)),
            pltpu.SemaphoreType.DMA((5,)),
            pltpu.SemaphoreType.DMA((5,)),
        ],
        compiler_params=pltpu.CompilerParams(
            vmem_limit_bytes=60000 * 1024, collective_id=0, has_side_effects=True
        ),
    )(latent, gain_one.reshape(1, chans), gain_two.reshape(1, chans),
      up_weight, conv_one, conv_two)
    return jnp.transpose(result, (0, 1, 3, 2))


def solution(mesh):
    return jax.shard_map(
        functools.partial(local, mesh.shape["ha"]),
        mesh=mesh,
        in_specs=(P("grp", "ha", None, "col"), P(), P(), P(), P(), P()),
        out_specs=P("grp", "ha", "col", None),
        check_vma=False,
    )
```

```python
import functools

import jax
import jax.numpy as jnp
from jax import lax
from jax.experimental import pallas as pl
from jax.experimental.pallas import tpu as pltpu
from jax.sharding import PartitionSpec as P

f32 = jnp.float32
bf16 = jnp.bfloat16
MESH = pl.DeviceIdType.MESH
STRIPS = 16
phase_taps = (((0, 1), (-1, 3)), ((0, 2), (1, 0)))


def activate(wide, half_gain):
    stats = jnp.sum(wide * wide, axis=-1, keepdims=True) * (1.0 / wide.shape[-1])
    half = wide * lax.rsqrt(stats + 1e-06) * half_gain
    return half * jnp.tanh(half) + half


def block_kernel(
    ha_count, lat, gain_one, gain_two, up_hbm, one_hbm, two_hbm, out,
    up_w, one_w, two_w, field, strips, ups, first, second, sem, send, recv
):
    ha = lax.axis_index("ha")
    col = lax.axis_index("col")
    share = lat.shape[2]
    chans = out.shape[2]
    rows, width = lat.shape[1], lat.shape[3]
    half = width // 2
    ql = half // STRIPS
    q = 2 * ql
    depth = 2 * share
    lead = 128
    tail = chans - lead
    mine = pl.ds(pl.multiple_of(col * share, share), share)
    other = {"col": 1 - col}
    has_above, has_below = ha > 0, ha < ha_count - 1

    barrier = pltpu.get_barrier_semaphore()
    pl.semaphore_signal(barrier, 1, device_id=other, device_id_type=MESH)

    @pl.when(has_above)
    def _():
        pl.semaphore_signal(barrier, 1, device_id={"ha": ha - 1}, device_id_type=MESH)

    @pl.when(has_below)
    def _():
        pl.semaphore_signal(barrier, 1, device_id={"ha": ha + 1}, device_id_type=MESH)

    own = pltpu.make_async_copy(lat.at[0], field.at[pl.ds(2, rows), mine], sem.at[3])
    own.start()

    copies = []
    for rp in range(2):
        for cp in range(2):
            tap = 0
            for _, ra in phase_taps[rp]:
                for _, cb in phase_taps[cp]:
                    copies.append(pltpu.make_async_copy(
                        up_hbm.at[ra, cb],
                        up_w.at[rp, cp, :, pl.ds(tap * depth, depth)],
                        sem.at[0],
                    ))
                    tap += 1
    for number, (src, dst) in enumerate(((one_hbm, one_w), (two_hbm, two_w))):
        for a in range(3):
            for b in range(3):
                at = a * 4 * lead + b * lead
                copies.append(pltpu.make_async_copy(
                    src.at[a, b, pl.ds(0, lead)], dst.at[pl.ds(at, lead)], sem.at[1 + number]
                ))
                at = a * 4 * lead + 3 * lead + b * tail if b < 2 else 12 * lead + a * tail
                copies.append(pltpu.make_async_copy(
                    src.at[a, b, pl.ds(lead, tail)], dst.at[pl.ds(at, tail)], sem.at[1 + number]
                ))
    for item in copies:
        item.start()

    peers = 1 + jnp.minimum(ha, 1) + jnp.minimum(ha_count - 1 - ha, 1)
    pl.semaphore_wait(barrier, peers)

    def remote(src, dst, target, n):
        return pltpu.make_async_remote_copy(
            src_ref=src, dst_ref=dst, send_sem=send.at[n], recv_sem=recv.at[n],
            device_id=target, device_id_type=MESH,
        )

    top, bottom = field.at[pl.ds(0, 2), mine], field.at[pl.ds(rows + 2, 2), mine]
    side = remote(lat.at[0], field.at[pl.ds(2, rows), mine], other, 0)
    down = remote(lat.at[0, pl.ds(rows - 2, 2)], top, {"ha": ha + 1}, 1)
    up = remote(lat.at[0, pl.ds(0, 2)], bottom, {"ha": ha - 1}, 2)
    pass_top = remote(top, top, other, 3)
    pass_bottom = remote(bottom, bottom, other, 4)

    @pl.when(has_below)
    def _():
        down.start()

    @pl.when(has_above)
    def _():
        up.start()

    side.start()

    for w in (one_w, two_w):
        w[pl.ds(12 * lead + 3 * tail, 2 * lead - 3 * tail)] = jnp.zeros(
            (2 * lead - 3 * tail, chans), bf16
        )
    for _, _, under in (first, second):
        last = under.shape[0] - 1
        under[last] = jnp.zeros(under.shape[1:], bf16)

    @pl.when(ha == 0)
    def _():
        field[pl.ds(0, 2)] = jnp.zeros((2, depth, width), bf16)

    @pl.when(ha == ha_count - 1)
    def _():
        field[pl.ds(rows + 2, 2)] = jnp.zeros((2, depth, width), bf16)

    strip = lax.broadcasted_iota(jnp.int32, (STRIPS, chans), 0)
    keep_low = (strip > 0) | (col > 0)
    keep_high = (strip < STRIPS - 1) | (col < 1)

    def keep(refs, r, t, value):
        ahead, next_col, next_row = refs
        value = value.astype(bf16)
        rest = value[:, lead:]
        ahead[r, t] = value[:, :lead]
        next_col[r, t + 1, :, pl.ds(0, tail)] = rest
        next_col[r, t, :, pl.ds(tail, tail)] = rest
        next_row[r + 1, t, :, pl.ds(0, tail)] = rest
        next_row[r, t, :, pl.ds(tail, tail)] = rest

    def windows(refs, start, count, cols):
        ahead, next_col, next_row = refs

        def flat(ref, r, t):
            return ref[pl.ds(r, count), pl.ds(t, cols)].reshape(count * cols * STRIPS, lead)

        pieces = []
        for a in range(3):
            pieces += [flat(ahead, start + a, b) for b in range(3)]
            pieces.append(flat(next_col, start + a, 1))
        pieces += [flat(next_row, start + 1, 2), flat(next_row, start + 3, 2)]
        return jnp.concatenate(pieces, axis=-1)

    count = (ql + 4) * STRIPS
    cell = lax.broadcasted_iota(jnp.int32, (count, width), 0)
    place = half * col + ql * (cell % STRIPS) + cell // STRIPS - 2
    pick = (place == lax.broadcasted_iota(jnp.int32, (count, width), 1)).astype(f32).astype(bf16)

    def pick_row(i, carry):
        chosen = lax.dot_general(
            pick, field[i], (((1,), (1,)), ((), ())), preferred_element_type=f32
        )
        strips[i] = chosen.astype(bf16).reshape(ql + 4, STRIPS, depth)
        return carry

    own.wait()
    side.wait()
    lax.fori_loop(2, rows + 2, pick_row, 0, unroll=4)

    half_one = gain_one[...] * 0.5
    half_two = gain_two[...] * 0.5

    for item in copies[:16]:
        item.wait()

    nt = ql + 2

    def upsample(groups, rp, cp):
        pieces = []
        for dr, _ in phase_taps[rp]:
            for dc, _ in phase_taps[cp]:
                parts = [
                    strips[pl.ds(start + 1 + dr, n), pl.ds(1 + dc, nt)].reshape(
                        n * nt * STRIPS, depth
                    )
                    for start, n in groups
                ]
                pieces.append(parts[0] if len(parts) == 1 else jnp.concatenate(parts, axis=0))
        lhs = jnp.concatenate(pieces, axis=-1)
        result = lax.dot_general(
            lhs, up_w[rp, cp], (((1,), (1,)), ((), ())), preferred_element_type=f32
        ).astype(bf16)
        act = activate(result.astype(f32), half_one)
        targets = [start + u for start, n in groups for u in range(n)]
        result = result.reshape(len(targets), nt, STRIPS, chans)
        act = act.reshape(len(targets), nt, STRIPS, chans)
        for u, target in enumerate(targets):
            for t in range(nt):
                value = act[u, t]
                if t == 0:
                    value = jnp.where(keep_low, value, 0.0)
                if t == nt - 1:
                    value = jnp.where(keep_high, value, 0.0)
                if target == 0:
                    value = jnp.where(has_above, value, 0.0)
                if target == rows + 1:
                    value = jnp.where(has_below, value, 0.0)
                ups[2 * target + rp, 2 * t + cp] = result[u, t]
                keep(first, 2 * target + rp, 2 * t + cp, value)

    inner = ((2, rows - 2),)
    outer = ((0, 2), (rows, 2))
    upsample(inner, 0, 0)
    upsample(inner, 0, 1)

    @pl.when(has_above)
    def _():
        down.wait_recv()
        pass_top.start()

    @pl.when(has_below)
    def _():
        up.wait_recv()
        pass_bottom.start()

    upsample(inner, 1, 0)
    upsample(inner, 1, 1)

    chunks = (2 * rows + 2) // 3
    for item in copies[16:34]:
        item.wait()

    def one_body(n, carry):
        count = 3
        lhs = windows(first, n * count, count, q + 2)
        hidden = jnp.dot(lhs, one_w[...], preferred_element_type=f32).astype(bf16)
        act = activate(hidden.astype(f32), half_two)
        act = act.reshape(count, q + 2, STRIPS, chans)
        for u in range(count):
            for t in range(q + 2):
                value = act[u, t]
                if t == 0:
                    value = jnp.where(keep_low, value, 0.0)
                if t == q + 1:
                    value = jnp.where(keep_high, value, 0.0)
                if u == 0:
                    value = jnp.where((n > 0) | has_above, value, 0.0)
                if u == count - 1:
                    value = jnp.where((n < chunks - 1) | has_below, value, 0.0)
                keep(second, n * count + u, t, value)
        return carry

    lax.fori_loop(2, chunks - 2, one_body, 0, unroll=2)

    @pl.when(has_above)
    def _():
        up.wait_send()
        pass_top.wait()

    @pl.when(has_below)
    def _():
        down.wait_send()
        pass_bottom.wait()

    lax.fori_loop(0, 2, pick_row, 0, unroll=2)
    lax.fori_loop(rows + 2, rows + 4, pick_row, 0, unroll=2)
    for rp in range(2):
        for cp in range(2):
            upsample(outer, rp, cp)

    lax.fori_loop(0, 2, one_body, 0, unroll=2)
    lax.fori_loop(chunks - 2, chunks, one_body, 0, unroll=2)

    for item in copies[34:]:
        item.wait()

    cell = lax.broadcasted_iota(jnp.int32, (q * STRIPS, width), 0)
    place = q * (cell % STRIPS) + cell // STRIPS
    put = (place == lax.broadcasted_iota(jnp.int32, (q * STRIPS, width), 1)).astype(f32).astype(bf16)

    def two_body(n, carry):
        count = 4
        lhs = windows(second, n * count, count, q)
        total = jnp.dot(lhs, two_w[...], preferred_element_type=f32)
        total = total.reshape(count, q * STRIPS, chans)
        for u in range(count):
            r = n * count + u
            skip = ups[r + 2, pl.ds(2, q)].reshape(q * STRIPS, chans).astype(f32)
            value = (total[u] + skip).astype(bf16)
            out[0, r] = lax.dot_general(
                value, put, (((0,), (0,)), ((), ())), preferred_element_type=f32
            ).astype(bf16)
        return carry

    lax.fori_loop(0, 2 * rows // 4, two_body, 0, unroll=2)


def packed(rows, cols):
    return [
        pltpu.VMEM((rows, cols, STRIPS, 128), bf16),
        pltpu.VMEM((rows, cols + 1, STRIPS, 128), bf16),
        pltpu.VMEM((rows + 1, cols, STRIPS, 128), bf16),
    ]


def local(ha_count, latent, up_weight, conv_one, gain_one, conv_two, gain_two):
    _, rows, width, share = latent.shape
    chans = conv_one.shape[3]
    ql = width // 2 // STRIPS
    q = 2 * ql
    latent = jnp.transpose(latent, (0, 1, 3, 2))
    up_weight = jnp.transpose(up_weight, (0, 1, 3, 2))
    anywhere = pl.BlockSpec(memory_space=pl.ANY)
    vmem = pl.BlockSpec(memory_space=pltpu.VMEM)
    result = pl.pallas_call(
        functools.partial(block_kernel, ha_count),
        out_shape=jax.ShapeDtypeStruct((1, 2 * rows, chans, width), bf16),
        in_specs=[anywhere] + [vmem] * 2 + [anywhere] * 3,
        out_specs=vmem,
        scratch_shapes=[
            pltpu.VMEM((2, 2, chans, 8 * share), bf16),
            pltpu.VMEM((14 * 128, chans), bf16),
            pltpu.VMEM((14 * 128, chans), bf16),
            pltpu.VMEM((rows + 4, 2 * share, width), bf16),
            pltpu.VMEM((rows + 4, ql + 4, STRIPS, 2 * share), bf16),
            pltpu.VMEM((2 * rows + 4, q + 4, STRIPS, chans), bf16),
            packed(2 * rows + 4, q + 4),
            packed(2 * rows + 2, q + 2),
            pltpu.SemaphoreType.DMA((4,)),
            pltpu.SemaphoreType.DMA((5,)),
            pltpu.SemaphoreType.DMA((5,)),
        ],
        compiler_params=pltpu.CompilerParams(
            vmem_limit_bytes=60000 * 1024, collective_id=0, has_side_effects=True
        ),
    )(latent, gain_one.reshape(1, chans), gain_two.reshape(1, chans),
      up_weight, conv_one, conv_two)
    return jnp.transpose(result, (0, 1, 3, 2))


def solution(mesh):
    return jax.shard_map(
        functools.partial(local, mesh.shape["ha"]),
        mesh=mesh,
        in_specs=(P("grp", "ha", None, "col"), P(), P(), P(), P(), P()),
        out_specs=P("grp", "ha", "col", None),
        check_vma=False,
    )
```
